1024 devices in a mesh: seq: 128 (over z, x, core), head: 8 (over y).
Axes of the slice: x: 8, y: 8, z: 8, core: 2. Of those that a mesh axis runs over, the one named last changes fastest.
Arguments:
- history: bfloat16 [98304, 1024], P('seq'), may hold values from -6 to 6
- ln_gain: bfloat16 [1024], replicated, may hold values from 0.5 to 1.5
- w_in: bfloat16 [4, 1024, 1024], P(None, None, 'head'), may hold values from -0.1875 to 0.1875
- out_gain: bfloat16 [1024], P('head'), may hold values from 0.5 to 1.5
- w_out: bfloat16 [1024, 1024], P('head'), may hold values from -0.25 to 0.25
- block_lists: int32 [768, 16], P('seq'), may hold values from 0 to 767, as said below
- counts: int32 [768], P('seq'), may hold values from 1 to 16, as said below
Outputs:
- mixed: bfloat16 [98304, 1024], P('seq', 'head')
The draws below stay inside these ranges and needn't reach their ends.
Inputs may be any that keep to these rules, and one draw needn't show every extreme that they name: For query block b, entries 0 to counts[b] - 1 of block_lists[b] are distinct blocks from max(0, b - 31) to b, and entry 0 is b itself; later entries equal b and are not live. counts[b] is at most min(16, b + 1); the last block has min(16, 32, 768) live entries.
All inputs are finite; a program needn't handle non-finite values.
Results may differ from the reference program's by a relative error of at most 0.008.
Values may be sent and summed in bfloat16 or wider, within the bound.
A program may use at most 64 MiB of HBM per device.

```python
import jax
import jax.numpy as jnp
from jax import lax

D = 1024
H = 8
DH = 128
BLK = 128
WIN = 32
MAXK = 16
TOK_DEV = 768
NBLK = 768
L = 98304


def pattern(key):
    base = jax.random.fold_in(key, 11)
    key_level, key_count, key_order = jax.random.split(base, 3)
    blocks_dev = TOK_DEV // BLK
    devices_seq = NBLK // blocks_dev
    block_ids = jnp.arange(NBLK, dtype=jnp.int32)
    window_avail = jnp.minimum(WIN, block_ids + 1)
    levels = jax.random.randint(key_level, (devices_seq,), MAXK // 2, MAXK + 1)
    level_rows = levels[block_ids // blocks_dev]
    counted = jax.random.randint(key_count, (NBLK,), (level_rows + 1) // 2, level_rows + 1)
    counted = jnp.minimum(counted, window_avail)
    counted = jnp.where(block_ids == NBLK - 1, jnp.minimum(MAXK, window_avail), counted)
    offsets = jnp.arange(1, WIN, dtype=jnp.int32)
    scores = jax.random.randint(key_order, (NBLK, WIN - 1), 0, 1 << 20) * WIN + offsets[None, :]
    scores = jnp.where(offsets[None, :] < window_avail[:, None], scores, scores + (1 << 26))
    order = jnp.argsort(scores, axis=1, stable=True)[:, :MAXK - 1].astype(jnp.int32) + 1
    picked = block_ids[:, None] - order
    slot_ids = jnp.arange(1, MAXK, dtype=jnp.int32)
    picked = jnp.where(slot_ids[None, :] < counted[:, None], picked, block_ids[:, None])
    listed = jnp.concatenate([block_ids[:, None], picked], axis=1)
    return (listed.astype(jnp.int32), counted.astype(jnp.int32))


def draw_block_lists(key, part):
    return pattern(key)[0]


def draw_counts(key, part):
    return pattern(key)[1]


def spiked(result, own_key, source, target, blocks, factor):
    owner, partner = [(jnp.arange(result.shape[axis_at]) // (result.shape[axis_at] // blocks)).reshape([-1 if axis == axis_at else 1 for axis in range(result.ndim)]) for axis_at in (source, target)]
    chosen = jax.random.permutation(own_key, blocks)[partner]
    strong = (owner == chosen) | (owner == (partner + blocks // 2) % blocks)
    return jnp.where(strong, factor * result, result)


def shard_levels(stream_key, dims, cuts, least, largest):
    factor_of, own = 1.0, jax.random.fold_in(stream_key, 6)
    for dim, blocks in cuts:
        draws = jnp.exp(jax.random.uniform(jax.random.fold_in(own, dim), (blocks,), jnp.float32, least / len(cuts), largest / len(cuts)))
        factor_of = factor_of * jnp.repeat(draws, dims[dim] // blocks).reshape([-1 if axis == dim else 1 for axis in range(len(dims))])
    return factor_of


def bell_draw(own_key, shape, scale, most, shards=(), held_as=jnp.bfloat16):
    drawn = jax.random.normal(own_key, shape, jnp.float32) * scale
    if len(shards) > 0:
        drawn = shard_levels(own_key, shape, shards, -0.22, 0.18) * drawn
    return jnp.clip(drawn, min=-most, max=most).astype(held_as)


def gaussian_with(rng, dims, spread, reach, cuts, heavy, kind=jnp.bfloat16):
    entries = spread * jax.random.normal(rng, dims, jnp.float32)
    if cuts:
        entries = entries * shard_levels(rng, dims, cuts, -0.22, 0.18)
    return jnp.clip(spiked(entries, jax.random.fold_in(rng, 3), *heavy), -reach, reach).astype(kind)


def setup_inputs(seed: int = 0) -> dict:
    key_of = jax.random.split(jax.random.key(seed), 8)
    history = bell_draw(key_of[0], (L, D), 1.0, 6.0, ((0, 128),))
    ln_gain = jnp.clip(jax.random.uniform(key_of[1], (D,), jnp.float32, 0.5, 1.5), 0.5, 1.5).astype(jnp.bfloat16)
    w_in = bell_draw(key_of[2], (4, D, H * DH), D ** -0.5, 0.1875, ((2, 8),))
    out_gain = jnp.clip(0.5 + 1.0 * jax.random.uniform(key_of[3], (H * DH,), jnp.float32) ** shard_levels(key_of[3], (H * DH,), ((0, 8),), -0.2, 0.2), 0.5, 1.5).astype(jnp.bfloat16)
    w_out = gaussian_with(key_of[4], (H * DH, D), (H * DH) ** -0.5, 0.25, ((0, 8),), (0, 1, 8, 2.0))
    block_lists = draw_block_lists(jax.random.fold_in(key_of[7], 71), 0)
    counts = draw_counts(jax.random.fold_in(key_of[7], 71), 0)
    return dict(history=history, ln_gain=ln_gain, w_in=w_in, out_gain=out_gain, w_out=w_out, block_lists=block_lists, counts=counts)


EPS = 1e-05

def reference(history, ln_gain, w_in, out_gain, w_out, block_lists, counts):
    floats = history.astype(jnp.float32)
    centre = lax.optimization_barrier(jnp.mean(floats, axis=-1, keepdims=True))
    spread_sq = lax.optimization_barrier(jnp.mean(jnp.square(floats - centre), axis=-1, keepdims=True))
    normed_x = ((floats - centre) * lax.rsqrt(spread_sq + EPS) * ln_gain.astype(jnp.float32)).astype(jnp.bfloat16)
    parts = [jax.nn.silu(jnp.dot(normed_x, w_in[which], preferred_element_type=jnp.float32)).astype(jnp.bfloat16) for which in range(4)]
    gating, values, queries, keys = parts
    key_blocks = keys.reshape(NBLK, BLK, H, DH)
    value_blocks = values.reshape(NBLK, BLK, H, DH)
    query_blocks = queries.reshape(NBLK, BLK, H, DH)
    positions = jnp.arange(BLK, dtype=jnp.int32)
    causal = positions[None, :] <= positions[:, None]
    scale = DH ** (-0.5)

    def one_block(block):
        listed = block_lists[block]
        in_list = jnp.arange(MAXK, dtype=jnp.int32) < counts[block]
        picked_keys = key_blocks[listed].astype(jnp.float32)
        picked_values = value_blocks[listed].astype(jnp.float32)
        query_here = query_blocks[block].astype(jnp.float32)
        scores = jnp.einsum('qhe,tkhe->hqtk', query_here, picked_keys) * scale
        allowed = in_list[None, :, None] & ((listed != block)[None, :, None] | causal[:, None, :])
        weights = jnp.where(allowed[None], jax.nn.silu(scores), 0.0).astype(jnp.bfloat16)
        weights = lax.optimization_barrier(weights).astype(jnp.float32)
        return jnp.einsum('hqtk,tkhe->qhe', weights, picked_values)
    attended = lax.map(one_block, jnp.arange(NBLK, dtype=jnp.int32)).reshape(NBLK * BLK, H, DH)
    centre_h = lax.optimization_barrier(jnp.mean(attended, axis=-1, keepdims=True))
    spread_h = lax.optimization_barrier(jnp.mean(jnp.square(attended - centre_h), axis=-1, keepdims=True))
    normed_h = (attended - centre_h) * lax.rsqrt(spread_h + EPS)
    gated = normed_h * out_gain.astype(jnp.float32).reshape(H, DH) * gating.astype(jnp.float32).reshape(NBLK * BLK, H, DH)
    gated = gated.astype(jnp.bfloat16).reshape(NBLK * BLK, H * DH)
    mixed = jnp.dot(gated, w_out, preferred_element_type=jnp.float32) + floats
    return mixed.astype(jnp.bfloat16)
```

```python
import functools

import jax
import jax.numpy as jnp
from jax import lax
from jax.experimental import pallas as pl
from jax.experimental.pallas import tpu as pltpu
from jax.sharding import PartitionSpec as P

DH = 128
BLK = 128
EPS = 1e-05
MESH = pl.DeviceIdType.MESH
F32 = jnp.float32
BF16 = jnp.bfloat16
NT = (((1,), (1,)), ((), ()))


def silu(v):
    half = 0.5 * v
    return half + half * jnp.tanh(half)


def kernel(
    S, Y, NB,
    hist, lng, win, og, wout, lists, o_ref,
    xb, nb, wkv, wqg, wf, kv, sv, qb, gb, att, mr, gat, gall, ob,
    in_sem, w_sem, xs, xr, ps, pr, rs, rr, ls, lr, bs, br, cs, cr, a1s, a1r, a2s, a2r,
):
    tok = NB * BLK
    rows_peer = tok // Y
    s = lax.axis_index("seq")
    h = lax.axis_index("head")
    p = lax.rem(s, 2)
    nxt = lax.rem(s + 2, S)
    prv = lax.rem(s + S - 2, S)
    sib = s + 1 - 2 * p
    scale = 0.5 * DH ** (-0.5)

    def block_rows(i):
        return pl.ds(pl.multiple_of(i * BLK, BLK), BLK)

    def load_block(i):
        return pltpu.make_async_copy(hist.at[block_rows(i)], xb.at[block_rows(i)], in_sem.at[i])

    def load_w(which, dst, half, sem):
        return pltpu.make_async_copy(
            win.at[which], dst.at[:, pl.ds(half * DH, DH)], w_sem.at[sem]
        )

    loads = [load_w(3, wkv, 0, 0), load_w(1, wkv, 1, 1), load_w(2, wqg, 0, 2), load_w(0, wqg, 1, 3)]
    half_rows = DH // 2
    load_out = pltpu.make_async_copy(wout, wf.at[h], w_sem.at[4])
    load_block(NB - 1).start()
    loads[0].start()
    loads[1].start()
    for i in range(NB - 2, -1, -1):
        load_block(i).start()
    loads[2].start()
    loads[3].start()
    load_out.start()

    barrier = pltpu.get_barrier_semaphore()
    for who in (nxt, prv, sib):
        pl.semaphore_signal(barrier, inc=1, device_id={"seq": who}, device_id_type=MESH)
    for k in range(1, Y):
        pl.semaphore_signal(
            barrier, inc=1, device_id={"head": lax.rem(h + k, Y)}, device_id_type=MESH
        )

    def hop(l, i):
        return pltpu.make_async_remote_copy(
            src_ref=kv.at[l, i], dst_ref=kv.at[l + 1, i],
            send_sem=xs.at[l, i], recv_sem=xr.at[l, i],
            device_id={"seq": nxt}, device_id_type=MESH,
        )

    def push(k, i):
        return pltpu.make_async_remote_copy(
            src_ref=kv.at[k + p, i], dst_ref=sv.at[k, i],
            send_sem=ps.at[k, i], recv_sem=pr.at[k, i],
            device_id={"seq": sib}, device_id_type=MESH,
        )

    up = lax.rem(h + 1, Y)
    down = lax.rem(h + Y - 1, Y)

    def ring_up(r):
        at = lax.rem(h - r + 1 + Y, Y)
        return pltpu.make_async_remote_copy(
            src_ref=wf.at[at, p], dst_ref=wf.at[at, p],
            send_sem=rs.at[r], recv_sem=rr.at[r],
            device_id={"head": up}, device_id_type=MESH,
        )

    def ring_down(r):
        at = lax.rem(h + r - 1, Y)
        return pltpu.make_async_remote_copy(
            src_ref=wf.at[at, p], dst_ref=wf.at[at, p],
            send_sem=ls.at[r], recv_sem=lr.at[r],
            device_id={"head": down}, device_id_type=MESH,
        )

    def share_up(r, half):
        at = lax.rem(h - r + Y, Y)
        return pltpu.make_async_remote_copy(
            src_ref=wf.at[at, half], dst_ref=wf.at[at, half],
            send_sem=bs.at[r], recv_sem=br.at[r],
            device_id={"seq": sib}, device_id_type=MESH,
        )

    def share_down(r, half):
        at = lax.rem(h + r, Y)
        return pltpu.make_async_remote_copy(
            src_ref=wf.at[at, half], dst_ref=wf.at[at, half],
            send_sem=cs.at[r], recv_sem=cr.at[r],
            device_id={"seq": sib}, device_id_type=MESH,
        )

    n_up = Y // 2
    n_down = Y - 1 - n_up

    def ring_step(n):
        @pl.when((n >= 1) & (n <= n_up))
        def _():
            ring_up(n).wait_recv()
            share_up(n, p).start()

        @pl.when((n >= 1) & (n <= n_down))
        def _():
            ring_down(n).wait_recv()
            share_down(n, p).start()

        @pl.when(n + 1 <= n_up)
        def _():
            ring_up(n + 1).start()

        @pl.when(n + 1 <= n_down)
        def _():
            ring_down(n + 1).start()

    loads[0].wait()
    loads[1].wait()
    gain = lng[...].astype(F32)

    def project(n, carry):
        i = NB - 1 - n
        load_block(i).wait()
        for piece in range(4):
            at = pl.ds(pl.multiple_of(i * BLK + piece * 32, 32), 32)
            floats = xb[at, :].astype(F32)
            centred = floats - jnp.mean(floats, axis=-1, keepdims=True)
            spread = jnp.mean(centred * centred, axis=-1, keepdims=True)
            nb[at, :] = (centred * lax.rsqrt(spread + EPS) * gain).astype(BF16)
        both = silu(jnp.dot(nb[block_rows(i), :], wkv[...], preferred_element_type=F32)).astype(BF16)
        kv[0, i, 0] = both[:, :DH]
        kv[0, i, 1] = both[:, DH:]

        @pl.when(n == 0)
        def _():
            pl.semaphore_wait(barrier, 3 + Y - 1)

        hop(0, i).start()

        @pl.when(p == 0)
        def _():
            push(0, i).start()

        return carry

    lax.fori_loop(0, NB, project, 0)
    load_out.wait()
    ring_step(0)

    loads[2].wait()
    loads[3].wait()

    def project_q(i, carry):
        both = silu(jnp.dot(nb[block_rows(i), :], wqg[...], preferred_element_type=F32)).astype(BF16)
        qb[block_rows(i), :] = both[:, :DH]
        gb[block_rows(i), :] = both[:, DH:]
        return carry

    lax.fori_loop(0, NB, project_q, 0)

    shape = mr.shape[1:]
    row = lax.broadcasted_iota(jnp.int32, shape, 0)
    lane = lax.broadcasted_iota(jnp.int32, shape, 1)
    back = (row * 11) >> 5
    key_id = NB * (s - back) + 2 * (row - 3 * back) + (lane >> 7)
    for j in range(NB):
        listed = key_id == lists[j, 0]
        for k in range(1, lists.shape[1]):
            listed = listed | (key_id == lists[j, k])
        mr[j] = jnp.where(listed, 1.0, 0.0)

    def attend(keys, values, at, first, t_own):
        m = (NB - first) * BLK
        scores = lax.dot_general(qb[first * BLK :, :], keys, NT, preferred_element_type=F32)
        pieces = []
        for j in range(first, NB):
            half = scores[(j - first) * BLK : (j - first + 1) * BLK] * scale
            keep = mr[j, pl.ds(at, 1), :]
            kept = half * keep
            weight = kept + kept * jnp.tanh(half)
            if t_own is not None and j <= 2 * t_own + 1:
                q_at = j * BLK + lax.broadcasted_iota(jnp.int32, weight.shape, 0)
                k_at = 2 * t_own * BLK + lax.broadcasted_iota(jnp.int32, weight.shape, 1)
                weight = jnp.where(k_at <= q_at, weight, 0.0)
            pieces.append(weight.astype(BF16))
        weights = jnp.concatenate(pieces, axis=0)
        update = jnp.dot(weights, values, preferred_element_type=F32)
        if t_own == 0:
            att[...] = update
        else:
            att[first * BLK :, :] += update

    def pair(buf, l, t):
        blocks = pl.ds(2 * t, 2)
        return buf[l, blocks, 0].reshape(2 * BLK, DH), buf[l, blocks, 1].reshape(2 * BLK, DH)

    for t in range(NB // 2):
        keys, values = pair(kv, 0, t)
        attend(keys, values, t, 2 * t, t)

    def middle(n, carry):
        l = 1 + n // 3
        t = 2 - lax.rem(n, 3)
        for i in (2 * t + 1, 2 * t):
            hop(l - 1, i).wait_recv()

            @pl.when((l == 1) | (p == 1) | (i == NB - 1))
            def _():
                hop(l, i).start()

            push(l - p, i).start()
        ring_step(n + 1)
        keys, values = pair(kv, l, t)
        attend(keys, values, 3 * (2 * l) + t, 0, None)
        for i in (2 * t + 1, 2 * t):
            push(l - 1, i).wait_recv()
        keys, values = pair(sv, l - 1, t)
        attend(keys, values, 3 * (2 * l - 1) + t, 0, None)
        return carry

    lax.fori_loop(0, 6, middle, 0)

    def last(n, carry):
        t = 2 - n
        for i in (2 * t + 1, 2 * t):

            @pl.when((p == 1) | (i == NB - 1))
            def _():
                hop(2, i).wait_recv()

            @pl.when(p == 1)
            def _():
                push(2, i).start()

        for i in (2 * t + 1, 2 * t):
            push(2, i).wait_recv()
        keys, values = pair(sv, 2, t)
        attend(keys, values, 3 * 5 + t, 0, None)
        return carry

    lax.fori_loop(0, 3, last, 0)

    scores = lax.dot_general(qb[:BLK, :], kv[3, NB - 1, 0], NT, preferred_element_type=F32)
    half = scores * scale
    kept = half * mr[0, 3 * 6 + 2 : 3 * 6 + 3, BLK:]
    weight = (kept + kept * jnp.tanh(half)).astype(BF16)
    att[:BLK, :] += jnp.dot(weight, kv[3, NB - 1, 1], preferred_element_type=F32)

    out_gain = og[...].astype(F32)
    for j in range(NB):
        at = slice(j * BLK, (j + 1) * BLK)
        floats = att[at, :]
        centred = floats - jnp.mean(floats, axis=-1, keepdims=True)
        spread = jnp.mean(centred * centred, axis=-1, keepdims=True)
        gat[at, :] = (
            centred * lax.rsqrt(spread + EPS) * out_gain * gb[at, :].astype(F32)
        ).astype(BF16)

    def share_rows(y):
        return pl.ds(pl.multiple_of(y * rows_peer, 32), rows_peer)

    def to_rows(k):
        peer = lax.rem(h + k, Y)
        return pltpu.make_async_remote_copy(
            src_ref=gat.at[share_rows(peer)], dst_ref=gall.at[h],
            send_sem=a1s.at[k], recv_sem=a1r.at[k],
            device_id={"head": peer}, device_id_type=MESH,
        )

    def to_columns(k):
        peer = lax.rem(h + k, Y)
        return pltpu.make_async_remote_copy(
            src_ref=ob.at[peer], dst_ref=o_ref.at[share_rows(h)],
            send_sem=a2s.at[k], recv_sem=a2r.at[k],
            device_id={"head": peer}, device_id_type=MESH,
        )

    for k in range(1, Y):
        to_rows(k).start()
    gall[h] = gat[share_rows(h), :]
    for r in range(1, n_up + 1):
        share_up(r, 1 - p).wait_recv()
    for r in range(1, n_down + 1):
        share_down(r, 1 - p).wait_recv()
    for k in range(1, Y):
        to_rows(k).wait_recv()
    gated = jnp.concatenate([gall[y] for y in range(Y)], axis=1)
    cols = ob.shape[2]
    for y in range(Y):
        at = slice(y * cols, (y + 1) * cols)
        weights = wf[:, :, :, at].reshape(Y * DH, cols)
        summed = jnp.dot(gated, weights, preferred_element_type=F32)
        ob[y] = (summed + xb[share_rows(h), at].astype(F32)).astype(BF16)
    for k in range(1, Y):
        to_columns(k).start()
    o_ref[share_rows(h), :] = ob[h]

    for l in range(2):
        for i in range(NB):
            hop(l, i).wait_send()
    for k in range(3):
        for i in range(NB):
            push(k, i).wait_send()
    hop(2, NB - 1).wait_send()

    @pl.when(p == 1)
    def _():
        for i in range(NB - 1):
            hop(2, i).wait_send()

    for r in range(1, n_up + 1):
        ring_up(r).wait_send()
        share_up(r, p).wait_send()
    for r in range(1, n_down + 1):
        ring_down(r).wait_send()
        share_down(r, p).wait_send()
    for k in range(1, Y):
        to_rows(k).wait_send()
        to_columns(k).wait_send()
        to_columns(k).wait_recv()


def solution(mesh):
    S, Y = mesh.shape["seq"], mesh.shape["head"]

    def body(history, ln_gain, w_in, out_gain, w_out, block_lists, counts):
        tok, width = history.shape
        NB = tok // BLK
        cols = width // Y
        vmem = pl.BlockSpec(memory_space=pltpu.VMEM)
        hbm = pl.BlockSpec(memory_space=pl.ANY)
        dma = pltpu.SemaphoreType.DMA
        return pl.pallas_call(
            functools.partial(kernel, S, Y, NB),
            out_shape=jax.ShapeDtypeStruct((tok, cols), BF16),
            in_specs=[hbm, vmem, hbm, vmem, hbm, pl.BlockSpec(memory_space=pltpu.SMEM)],
            out_specs=vmem,
            scratch_shapes=[
                pltpu.VMEM((tok, width), BF16),
                pltpu.VMEM((tok, width), BF16),
                pltpu.VMEM((width, 2 * DH), BF16),
                pltpu.VMEM((width, 2 * DH), BF16),
                pltpu.VMEM((Y, 2, DH // 2, width), BF16),
                pltpu.VMEM((4, NB, 2, BLK, DH), BF16),
                pltpu.VMEM((3, NB, 2, BLK, DH), BF16),
                pltpu.VMEM((tok, DH), BF16),
                pltpu.VMEM((tok, DH), BF16),
                pltpu.VMEM((tok, DH), F32),
                pltpu.VMEM((NB, 24, 2 * BLK), F32),
                pltpu.VMEM((tok, DH), BF16),
                pltpu.VMEM((Y, tok // Y, DH), BF16),
                pltpu.VMEM((Y, tok // Y, cols), BF16),
                dma((NB,)), dma((5,)),
                dma((3, NB)), dma((3, NB)), dma((3, NB)), dma((3, NB)),
                dma((Y,)), dma((Y,)), dma((Y,)), dma((Y,)),
                dma((Y,)), dma((Y,)), dma((Y,)), dma((Y,)),
                dma((Y,)), dma((Y,)), dma((Y,)), dma((Y,)),
            ],
            compiler_params=pltpu.CompilerParams(
                collective_id=0, has_side_effects=True, vmem_limit_bytes=56 * 2**20
            ),
        )(
            history, ln_gain.reshape(1, width), w_in, out_gain.reshape(1, DH),
            w_out.reshape(2, DH // 2, width), block_lists,
        )

    placed = (
        P("seq", None),
        P(),
        P(None, None, "head"),
        P("head"),
        P("head", None),
        P("seq", None),
        P("seq"),
    )
    return jax.shard_map(
        body, mesh=mesh, in_specs=placed, out_specs=P("seq", "head"), check_vma=False
    )
```

```python
import functools

import jax
import jax.numpy as jnp
from jax import lax
from jax.experimental import pallas as pl
from jax.experimental.pallas import tpu as pltpu
from jax.sharding import PartitionSpec as P

DH = 128
BLK = 128
EPS = 1e-05
MESH = pl.DeviceIdType.MESH
F32 = jnp.float32
BF16 = jnp.bfloat16
NT = (((1,), (1,)), ((), ()))


def silu(v):
    half = 0.5 * v
    return half + half * jnp.tanh(half)


def kernel(
    S, Y, NB,
    hist, lng, win, og, wout, lists, o_ref,
    xb, nb, wkv, wqg, wf, kv, sv, qb, gb, att, mr, gat, gall, ob,
    in_sem, w_sem, xs, xr, ps, pr, rs, rr, ls, lr, bs, br, cs, cr, a1s, a1r, a2s, a2r,
):
    share = BLK // Y
    s = lax.axis_index("seq")
    h = lax.axis_index("head")
    p = lax.rem(s, 2)
    chip = lax.div(s, 2)
    is_first, is_last = chip == 0, chip == S // 2 - 1
    nxt = jnp.minimum(s + 2, S - 1)
    prv = jnp.maximum(s - 2, 0)
    sib = s + 1 - 2 * p
    scale = 0.5 * DH ** (-0.5)

    def block_rows(i):
        return pl.ds(pl.multiple_of(i * BLK, BLK), BLK)

    def load_block(i):
        return pltpu.make_async_copy(hist.at[block_rows(i)], xb.at[block_rows(i)], in_sem.at[i])

    def load_w(which, dst, half, sem):
        return pltpu.make_async_copy(
            win.at[which], dst.at[:, pl.ds(half * DH, DH)], w_sem.at[sem]
        )

    loads = [load_w(3, wkv, 0, 0), load_w(1, wkv, 1, 1), load_w(2, wqg, 0, 2), load_w(0, wqg, 1, 3)]
    half_rows = DH // 2
    load_out = pltpu.make_async_copy(wout, wf.at[h], w_sem.at[4])
    load_block(NB - 1).start()
    loads[0].start()
    loads[1].start()
    for i in range(NB - 2, -1, -1):
        load_block(i).start()
    loads[2].start()
    loads[3].start()
    load_out.start()

    barrier = pltpu.get_barrier_semaphore()
    pl.semaphore_signal(barrier, inc=1, device_id={"seq": sib}, device_id_type=MESH)

    @pl.when(~is_last)
    def _():
        pl.semaphore_signal(barrier, inc=1, device_id={"seq": nxt}, device_id_type=MESH)

    @pl.when(~is_first)
    def _():
        pl.semaphore_signal(barrier, inc=1, device_id={"seq": prv}, device_id_type=MESH)

    for k in range(1, Y):
        pl.semaphore_signal(
            barrier, inc=1, device_id={"head": lax.rem(h + k, Y)}, device_id_type=MESH
        )

    def hop(l, i):
        return pltpu.make_async_remote_copy(
            src_ref=kv.at[l, i], dst_ref=kv.at[l + 1, i],
            send_sem=xs.at[l, i], recv_sem=xr.at[l, i],
            device_id={"seq": nxt}, device_id_type=MESH,
        )

    def push(k, i):
        return pltpu.make_async_remote_copy(
            src_ref=kv.at[k + p, i], dst_ref=sv.at[k, i],
            send_sem=ps.at[k, i], recv_sem=pr.at[k, i],
            device_id={"seq": sib}, device_id_type=MESH,
        )

    up = lax.rem(h + 1, Y)
    down = lax.rem(h + Y - 1, Y)

    def ring_up(r):
        at = lax.rem(h - r + 1 + Y, Y)
        return pltpu.make_async_remote_copy(
            src_ref=wf.at[at, p], dst_ref=wf.at[at, p],
            send_sem=rs.at[r], recv_sem=rr.at[r],
            device_id={"head": up}, device_id_type=MESH,
        )

    def ring_down(r):
        at = lax.rem(h + r - 1, Y)
        return pltpu.make_async_remote_copy(
            src_ref=wf.at[at, p], dst_ref=wf.at[at, p],
            send_sem=ls.at[r], recv_sem=lr.at[r],
            device_id={"head": down}, device_id_type=MESH,
        )

    def share_up(r, half):
        at = lax.rem(h - r + Y, Y)
        return pltpu.make_async_remote_copy(
            src_ref=wf.at[at, half], dst_ref=wf.at[at, half],
            send_sem=bs.at[r], recv_sem=br.at[r],
            device_id={"seq": sib}, device_id_type=MESH,
        )

    def share_down(r, half):
        at = lax.rem(h + r, Y)
        return pltpu.make_async_remote_copy(
            src_ref=wf.at[at, half], dst_ref=wf.at[at, half],
            send_sem=cs.at[r], recv_sem=cr.at[r],
            device_id={"seq": sib}, device_id_type=MESH,
        )

    n_up = Y // 2
    n_down = Y - 1 - n_up

    def ring_step(n):
        @pl.when((n >= 1) & (n <= n_up))
        def _():
            ring_up(n).wait_recv()
            share_up(n, p).start()

        @pl.when((n >= 1) & (n <= n_down))
        def _():
            ring_down(n).wait_recv()
            share_down(n, p).start()

        @pl.when(n + 1 <= n_up)
        def _():
            ring_up(n + 1).start()

        @pl.when(n + 1 <= n_down)
        def _():
            ring_down(n + 1).start()

    loads[0].wait()
    loads[1].wait()
    gain = lng[...].astype(F32).reshape(1, -1)

    def project(n, carry):
        i = NB - 1 - n
        load_block(i).wait()
        for piece in range(4):
            at = pl.ds(pl.multiple_of(i * BLK + piece * 32, 32), 32)
            floats = xb[at, :].astype(F32)
            centred = floats - jnp.mean(floats, axis=-1, keepdims=True)
            spread = jnp.mean(centred * centred, axis=-1, keepdims=True)
            nb[at, :] = (centred * lax.rsqrt(spread + EPS) * gain).astype(BF16)
        both = silu(jnp.dot(nb[block_rows(i), :], wkv[...], preferred_element_type=F32)).astype(BF16)
        kv[0, i, 0] = both[:, :DH]
        kv[0, i, 1] = both[:, DH:]

        @pl.when(n == 0)
        def _():
            pl.semaphore_wait(barrier, Y + (chip > 0).astype(jnp.int32) + (chip < S // 2 - 1).astype(jnp.int32))

        @pl.when(~is_last)
        def _():
            hop(0, i).start()

        @pl.when(p == 0)
        def _():
            push(0, i).start()

        return carry

    lax.fori_loop(0, NB, project, 0)
    load_out.wait()
    ring_step(0)

    loads[2].wait()
    loads[3].wait()

    def project_q(i, carry):
        both = silu(jnp.dot(nb[block_rows(i), :], wqg[...], preferred_element_type=F32)).astype(BF16)
        qb[block_rows(i), :] = both[:, :DH]
        gb[block_rows(i), :] = both[:, DH:]
        return carry

    lax.fori_loop(0, NB, project_q, 0)

    shape = mr.shape[1:]
    row = lax.broadcasted_iota(jnp.int32, shape, 0)
    lane = lax.broadcasted_iota(jnp.int32, shape, 1)
    back = (row * 11) >> 5
    key_id = NB * (s - back) + 2 * (row - 3 * back) + (lane >> 7)
    for j in range(NB):
        listed = key_id == lists[j, 0]
        for k in range(1, lists.shape[1]):
            listed = listed | (key_id == lists[j, k])
        mr[j] = jnp.where(listed, 1.0, 0.0)

    def attend(keys, values, at, first, t_own):
        m = (NB - first) * BLK
        scores = lax.dot_general(qb[first * BLK :, :], keys, NT, preferred_element_type=F32)
        pieces = []
        for j in range(first, NB):
            half = scores[(j - first) * BLK : (j - first + 1) * BLK] * scale
            keep = mr[j, pl.ds(at, 1), :]
            kept = half * keep
            weight = kept + kept * jnp.tanh(half)
            if t_own is not None and j <= 2 * t_own + 1:
                q_at = j * BLK + lax.broadcasted_iota(jnp.int32, weight.shape, 0)
                k_at = 2 * t_own * BLK + lax.broadcasted_iota(jnp.int32, weight.shape, 1)
                weight = jnp.where(k_at <= q_at, weight, 0.0)
            pieces.append(weight.astype(BF16))
        weights = jnp.concatenate(pieces, axis=0)
        update = jnp.dot(weights, values, preferred_element_type=F32)
        if t_own == 0:
            att[...] = update
        else:
            att[first * BLK :, :] += update

    def pair(buf, l, t):
        blocks = pl.ds(2 * t, 2)
        return buf[l, blocks, 0].reshape(2 * BLK, DH), buf[l, blocks, 1].reshape(2 * BLK, DH)

    for t in range(NB // 2):
        keys, values = pair(kv, 0, t)
        attend(keys, values, t, 2 * t, t)

    def has_lane(l):
        return chip >= l

    def has_shared(k):
        return chip + p >= k + 1

    def middle(n, carry):
        l = 1 + n // 3
        t = 2 - lax.rem(n, 3)

        @pl.when(has_lane(l))
        def _():
            for i in (2 * t + 1, 2 * t):
                hop(l - 1, i).wait_recv()

                @pl.when(((l == 1) | (p == 1) | (i == NB - 1)) & ~is_last)
                def _():
                    hop(l, i).start()

                push(l - p, i).start()

        ring_step(n + 1)

        @pl.when(has_lane(l))
        def _():
            keys, values = pair(kv, l, t)
            attend(keys, values, 3 * (2 * l) + t, 0, None)

        @pl.when(has_shared(l - 1))
        def _():
            for i in (2 * t + 1, 2 * t):
                push(l - 1, i).wait_recv()
            keys, values = pair(sv, l - 1, t)
            attend(keys, values, 3 * (2 * l - 1) + t, 0, None)

        return carry

    lax.fori_loop(0, 6, middle, 0)

    def take_third(i):
        @pl.when(has_lane(3) & (p == 1))
        def _():
            hop(2, i).wait_recv()
            push(2, i).start()

    def attend_shared(t):
        @pl.when(has_shared(2))
        def _():
            for i in (2 * t + 1, 2 * t):
                push(2, i).wait_recv()
            keys, values = pair(sv, 2, t)
            attend(keys, values, 3 * 5 + t, 0, None)

    half_blocks = NB // 2

    def some(part):
        return pl.ds(part * half_blocks, half_blocks)

    def to_rows(part, k):
        peer = lax.rem(h + k, Y)
        return pltpu.make_async_remote_copy(
            src_ref=gat.at[some(part), peer], dst_ref=gall.at[h, some(part)],
            send_sem=a1s.at[part, k], recv_sem=a1r.at[part, k],
            device_id={"head": peer}, device_id_type=MESH,
        )

    def to_columns(part, k):
        peer = lax.rem(h + k, Y)
        return pltpu.make_async_remote_copy(
            src_ref=ob.at[peer, some(part)], dst_ref=o_ref.at[some(part), h],
            send_sem=a2s.at[part, k], recv_sem=a2r.at[part, k],
            device_id={"head": peer}, device_id_type=MESH,
        )

    def keep_columns(part):
        return pltpu.make_async_copy(ob.at[h, some(part)], o_ref.at[some(part), h], a2r.at[part, 0])

    far_first = sorted(range(1, Y), key=lambda k: -min(k, Y - k))
    out_gain = og[...].astype(F32).reshape(1, -1)

    def finish(part):
        for j in range(part * half_blocks, (part + 1) * half_blocks):
            at = slice(j * BLK, (j + 1) * BLK)
            floats = att[at, :]
            centred = floats - jnp.mean(floats, axis=-1, keepdims=True)
            spread = jnp.mean(centred * centred, axis=-1, keepdims=True)
            normed = centred * lax.rsqrt(spread + EPS) * out_gain * gb[at, :].astype(F32)
            gat[j] = normed.astype(BF16).reshape(Y, share, DH)
        for k in far_first:
            to_rows(part, k).start()
        gall[h, some(part)] = gat[some(part), h]

    def mix(part):
        for k in far_first:
            to_rows(part, k).wait_recv()
        rows = half_blocks * share
        gated = jnp.concatenate(
            [gall[y, some(part)].reshape(rows, DH) for y in range(Y)], axis=1
        )
        cols = ob.shape[3]
        for y in range(Y):
            at = slice(y * cols, (y + 1) * cols)
            weights = wf[:, :, :, at].reshape(Y * DH, cols)
            summed = jnp.dot(gated, weights, preferred_element_type=F32)
            for n in range(half_blocks):
                j = part * half_blocks + n
                mine = pl.ds(pl.multiple_of(j * BLK + h * share, share), share)
                ob[y, j] = (
                    summed[n * share : (n + 1) * share] + xb[mine, at].astype(F32)
                ).astype(BF16)
        for k in far_first:
            to_columns(part, k).start()
        keep_columns(part).start()

    take_third(5)
    attend_shared(2)
    take_third(4)
    attend_shared(1)
    finish(1)
    take_third(3)
    take_third(2)
    attend_shared(0)

    @pl.when(has_lane(3))
    def _():
        @pl.when(p == 0)
        def _():
            hop(2, NB - 1).wait_recv()

        scores = lax.dot_general(qb[:BLK, :], kv[3, NB - 1, 0], NT, preferred_element_type=F32)
        half = scores * scale
        kept = half * mr[0, 3 * 6 + 2 : 3 * 6 + 3, BLK:]
        weight = (kept + kept * jnp.tanh(half)).astype(BF16)
        att[:BLK, :] += jnp.dot(weight, kv[3, NB - 1, 1], preferred_element_type=F32)

    finish(0)
    take_third(1)
    take_third(0)
    for r in range(1, n_up + 1):
        share_up(r, 1 - p).wait_recv()
    for r in range(1, n_down + 1):
        share_down(r, 1 - p).wait_recv()
    mix(1)
    mix(0)

    for l in range(3):

        @pl.when(has_lane(l) & ~is_last)
        def _():
            for i in range(NB):
                if l < 2 or i == NB - 1:
                    hop(l, i).wait_send()
                else:

                    @pl.when(p == 1)
                    def _():
                        hop(l, i).wait_send()

        @pl.when(has_lane(l + p))
        def _():
            for i in range(NB):
                push(l, i).wait_send()

    for r in range(1, n_up + 1):
        ring_up(r).wait_send()
        share_up(r, p).wait_send()
    for r in range(1, n_down + 1):
        ring_down(r).wait_send()
        share_down(r, p).wait_send()
    for part in range(2):
        keep_columns(part).wait()
        for k in range(1, Y):
            to_rows(part, k).wait_send()
            to_columns(part, k).wait_send()
            to_columns(part, k).wait_recv()


def solution(mesh):
    S, Y = mesh.shape["seq"], mesh.shape["head"]

    def body(history, ln_gain, w_in, out_gain, w_out, block_lists, counts):
        tok, width = history.shape
        NB = tok // BLK
        cols = width // Y
        vmem = pl.BlockSpec(memory_space=pltpu.VMEM)
        hbm = pl.BlockSpec(memory_space=pltpu.HBM)
        dma = pltpu.SemaphoreType.DMA
        return pl.pallas_call(
            functools.partial(kernel, S, Y, NB),
            out_shape=jax.ShapeDtypeStruct((NB, Y, BLK // Y, cols), BF16),
            in_specs=[hbm, vmem, hbm, vmem, hbm, pl.BlockSpec(memory_space=pltpu.SMEM)],
            out_specs=hbm,
            scratch_shapes=[
                pltpu.VMEM((tok, width), BF16),
                pltpu.VMEM((tok, width), BF16),
                pltpu.VMEM((width, 2 * DH), BF16),
                pltpu.VMEM((width, 2 * DH), BF16),
                pltpu.VMEM((Y, 2, DH // 2, width), BF16),
                pltpu.VMEM((4, NB, 2, BLK, DH), BF16),
                pltpu.VMEM((3, NB, 2, BLK, DH), BF16),
                pltpu.VMEM((tok, DH), BF16),
                pltpu.VMEM((tok, DH), BF16),
                pltpu.VMEM((tok, DH), F32),
                pltpu.VMEM((NB, 24, 2 * BLK), F32),
                pltpu.VMEM((NB, Y, BLK // Y, DH), BF16),
                pltpu.VMEM((Y, NB, BLK // Y, DH), BF16),
                pltpu.VMEM((Y, NB, BLK // Y, cols), BF16),
                dma((NB,)), dma((5,)),
                dma((3, NB)), dma((3, NB)), dma((3, NB)), dma((3, NB)),
                dma((Y,)), dma((Y,)), dma((Y,)), dma((Y,)),
                dma((Y,)), dma((Y,)), dma((Y,)), dma((Y,)),
                dma((2, Y)), dma((2, Y)), dma((2, Y)), dma((2, Y)),
            ],
            compiler_params=pltpu.CompilerParams(
                collective_id=0, has_side_effects=True, vmem_limit_bytes=56 * 2**20
            ),
        )(
            history, ln_gain, w_in, out_gain,
            w_out.reshape(2, DH // 2, width), block_lists,
        ).reshape(tok, cols)

    placed = (
        P("seq", None),
        P(),
        P(None, None, "head"),
        P("head"),
        P("head", None),
        P("seq", None),
        P("seq"),
    )
    return jax.shard_map(
        body, mesh=mesh, in_specs=placed, out_specs=P("seq", "head"), check_vma=False
    )
```

```python
import functools

import jax
import jax.numpy as jnp
from jax import lax
from jax.experimental import pallas as pl
from jax.experimental.pallas import tpu as pltpu
from jax.sharding import PartitionSpec as P

DH = 128
BLK = 128
EPS = 1e-05
MESH = pl.DeviceIdType.MESH
F32 = jnp.float32
BF16 = jnp.bfloat16
NT = (((1,), (1,)), ((), ()))


def silu(v):
    half = 0.5 * v
    return half + half * jnp.tanh(half)


def kernel(
    S, Y, NB,
    hist, lng, win, og, wout, lists, o_ref,
    xb, nb, wkv, wqg, wf, kv, sv, qb, gb, att, mr, gat, gall, ob,
    in_sem, w_sem, xs, xr, ps, pr, rs, rr, ls, lr, bs, br, cs, cr, a1s, a1r, a2s, a2r, fs,
):
    share = BLK // Y
    s = lax.axis_index("seq")
    h = lax.axis_index("head")
    p = lax.rem(s, 2)
    chip = lax.div(s, 2)
    is_first, is_last = chip == 0, chip == S // 2 - 1
    nxt = jnp.minimum(s + 2, S - 1)
    prv = jnp.maximum(s - 2, 0)
    sib = s + 1 - 2 * p
    scale = 0.5 * DH ** (-0.5)

    def block_rows(i):
        return pl.ds(pl.multiple_of(i * BLK, BLK), BLK)

    def load_block(i):
        return pltpu.make_async_copy(hist.at[block_rows(i)], xb.at[block_rows(i)], in_sem.at[i])

    def load_w(which, dst, half, sem):
        return pltpu.make_async_copy(
            win.at[which], dst.at[:, pl.ds(half * DH, DH)], w_sem.at[sem]
        )

    loads = [load_w(3, wkv, 0, 0), load_w(1, wkv, 1, 1), load_w(2, wqg, 0, 2), load_w(0, wqg, 1, 3)]
    half_rows = DH // 2
    load_out = pltpu.make_async_copy(wout, wf.at[h], w_sem.at[4])
    load_block(NB - 1).start()
    loads[0].start()
    loads[1].start()
    load_out.start()
    for i in range(NB - 2, -1, -1):
        load_block(i).start()
    loads[2].start()
    loads[3].start()

    barrier = pltpu.get_barrier_semaphore()
    pl.semaphore_signal(barrier, inc=1, device_id={"seq": sib}, device_id_type=MESH)

    @pl.when(~is_first)
    def _():
        pl.semaphore_signal(barrier, inc=1, device_id={"seq": prv}, device_id_type=MESH)

    @pl.when(~is_first & (p == 0))
    def _():
        pl.semaphore_signal(
            barrier, inc=1, device_id={"seq": jnp.maximum(s - 1, 0)}, device_id_type=MESH
        )

    for k in range(1, Y):
        pl.semaphore_signal(
            barrier, inc=1, device_id={"head": lax.rem(h + k, Y)}, device_id_type=MESH
        )

    def hop(l, i):
        return pltpu.make_async_remote_copy(
            src_ref=kv.at[l, i], dst_ref=kv.at[l + 1, i],
            send_sem=xs.at[l, i], recv_sem=xr.at[l, i],
            device_id={"seq": nxt}, device_id_type=MESH,
        )

    def push(k, i):
        return pltpu.make_async_remote_copy(
            src_ref=kv.at[k + p, i], dst_ref=sv.at[k, i],
            send_sem=ps.at[k, i], recv_sem=pr.at[k, i],
            device_id={"seq": sib}, device_id_type=MESH,
        )

    def third(i):
        return pltpu.make_async_remote_copy(
            src_ref=kv.at[2, i], dst_ref=sv.at[2, i],
            send_sem=xs.at[2, i], recv_sem=pr.at[2, i],
            device_id={"seq": jnp.minimum(s + 1, S - 1)}, device_id_type=MESH,
        )

    third_shared = pltpu.make_async_remote_copy(
        src_ref=sv.at[2, NB - 1], dst_ref=kv.at[3, NB - 1],
        send_sem=fs.at[0], recv_sem=xr.at[2, NB - 1],
        device_id={"seq": sib}, device_id_type=MESH,
    )

    up = lax.rem(h + 1, Y)
    down = lax.rem(h + Y - 1, Y)

    def ring_up(r):
        at = lax.rem(h - r + 1 + Y, Y)
        return pltpu.make_async_remote_copy(
            src_ref=wf.at[at, p], dst_ref=wf.at[at, p],
            send_sem=rs.at[r], recv_sem=rr.at[r],
            device_id={"head": up}, device_id_type=MESH,
        )

    def ring_down(r):
        at = lax.rem(h + r - 1, Y)
        return pltpu.make_async_remote_copy(
            src_ref=wf.at[at, p], dst_ref=wf.at[at, p],
            send_sem=ls.at[r], recv_sem=lr.at[r],
            device_id={"head": down}, device_id_type=MESH,
        )

    def share_up(r, half):
        at = lax.rem(h - r + Y, Y)
        return pltpu.make_async_remote_copy(
            src_ref=wf.at[at, half], dst_ref=wf.at[at, half],
            send_sem=bs.at[r], recv_sem=br.at[r],
            device_id={"seq": sib}, device_id_type=MESH,
        )

    def share_down(r, half):
        at = lax.rem(h + r, Y)
        return pltpu.make_async_remote_copy(
            src_ref=wf.at[at, half], dst_ref=wf.at[at, half],
            send_sem=cs.at[r], recv_sem=cr.at[r],
            device_id={"seq": sib}, device_id_type=MESH,
        )

    n_up = Y // 2
    n_down = Y - 1 - n_up

    def ring_step(n):
        @pl.when((n >= 1) & (n <= n_up))
        def _():
            ring_up(n).wait_recv()
            share_up(n, p).start()

        @pl.when((n >= 1) & (n <= n_down))
        def _():
            ring_down(n).wait_recv()
            share_down(n, p).start()

        @pl.when(n + 1 <= n_up)
        def _():
            ring_up(n + 1).start()

        @pl.when(n + 1 <= n_down)
        def _():
            ring_down(n + 1).start()

    loads[0].wait()
    loads[1].wait()
    gain = lng[...].astype(F32).reshape(1, -1)

    def project(n, carry):
        i = NB - 1 - n
        load_block(i).wait()
        for piece in range(4):
            at = pl.ds(pl.multiple_of(i * BLK + piece * 32, 32), 32)
            floats = xb[at, :].astype(F32)
            centred = floats - jnp.mean(floats, axis=-1, keepdims=True)
            spread = jnp.mean(centred * centred, axis=-1, keepdims=True)
            nb[at, :] = (centred * lax.rsqrt(spread + EPS) * gain).astype(BF16)
        both = silu(jnp.dot(nb[block_rows(i), :], wkv[...], preferred_element_type=F32)).astype(BF16)
        kv[0, i, 0] = both[:, :DH]
        kv[0, i, 1] = both[:, DH:]

        @pl.when(n == 0)
        def _():
            pl.semaphore_wait(barrier, Y + (chip < S // 2 - 1).astype(jnp.int32) * (1 + p))

        @pl.when(~is_last)
        def _():
            hop(0, i).start()

        @pl.when(p == 0)
        def _():
            push(0, i).start()

        @pl.when(n == 0)
        def _():
            load_out.wait()
            ring_step(0)

        return carry

    lax.fori_loop(0, NB, project, 0)

    loads[2].wait()
    loads[3].wait()

    def project_q(i, carry):
        both = silu(jnp.dot(nb[block_rows(i), :], wqg[...], preferred_element_type=F32)).astype(BF16)
        qb[block_rows(i), :] = both[:, :DH]
        gb[block_rows(i), :] = both[:, DH:]
        return carry

    lax.fori_loop(0, NB, project_q, 0)

    shape = mr.shape[1:]
    row = lax.broadcasted_iota(jnp.int32, shape, 0)
    lane = lax.broadcasted_iota(jnp.int32, shape, 1)
    back = (row * 11) >> 5
    key_id = NB * (s - back) + 2 * (row - 3 * back) + (lane >> 7)
    for j in range(NB):
        listed = key_id == lists[j, 0]
        for k in range(1, lists.shape[1]):
            listed = listed | (key_id == lists[j, k])
        mr[j] = jnp.where(listed, 1.0, 0.0)

    def attend(keys, values, at, first, t_own):
        scores = lax.dot_general(qb[first * BLK :, :], keys, NT, preferred_element_type=F32)
        pieces = []
        for j in range(first, NB):
            half = scores[(j - first) * BLK : (j - first + 1) * BLK] * scale
            keep = mr[j, pl.ds(at, 1), :]
            kept = half * keep
            weight = kept + kept * jnp.tanh(half)
            if t_own is not None and j <= 2 * t_own + 1:
                q_at = j * BLK + lax.broadcasted_iota(jnp.int32, weight.shape, 0)
                k_at = 2 * t_own * BLK + lax.broadcasted_iota(jnp.int32, weight.shape, 1)
                weight = jnp.where(k_at <= q_at, weight, 0.0)
            pieces.append(weight.astype(BF16))
        weights = jnp.concatenate(pieces, axis=0)
        update = jnp.dot(weights, values, preferred_element_type=F32)
        if t_own == 0:
            att[...] = update
        else:
            att[first * BLK :, :] += update

    def pair(buf, l, t):
        blocks = pl.ds(2 * t, 2)
        return buf[l, blocks, 0].reshape(2 * BLK, DH), buf[l, blocks, 1].reshape(2 * BLK, DH)

    for t in range(NB // 2):
        keys, values = pair(kv, 0, t)
        attend(keys, values, t, 2 * t, t)

    def has_lane(l):
        return chip >= l

    def has_shared(k):
        return chip + p >= k + 1

    def middle(n, carry):
        l = 1 + n // 3
        t = 2 - lax.rem(n, 3)

        @pl.when(has_lane(l))
        def _():
            for i in (2 * t + 1, 2 * t):
                hop(l - 1, i).wait_recv()

                @pl.when(((l == 1) | ((p == 0) & (i == NB - 1))) & ~is_last)
                def _():
                    hop(l, i).start()

                @pl.when((l == 2) & (p == 1) & ~is_last)
                def _():
                    third(i).start()

                push(l - p, i).start()


        @pl.when(has_lane(l))
        def _():
            keys, values = pair(kv, l, t)
            attend(keys, values, 3 * (2 * l) + t, 0, None)

        @pl.when(has_shared(l - 1))
        def _():
            for i in (2 * t + 1, 2 * t):
                push(l - 1, i).wait_recv()
            keys, values = pair(sv, l - 1, t)
            attend(keys, values, 3 * (2 * l - 1) + t, 0, None)

        @pl.when(lax.rem(n, 2) == 1)
        def _():
            ring_step((n + 1) // 2)

        return carry

    lax.fori_loop(0, 6, middle, 0)

    def attend_shared(t):
        @pl.when(has_shared(2))
        def _():
            for i in (2 * t + 1, 2 * t):
                push(2, i).wait_recv()
                if i == NB - 1:

                    @pl.when(p == 0)
                    def _():
                        third_shared.start()

            keys, values = pair(sv, 2, t)
            attend(keys, values, 3 * 5 + t, 0, None)

    half_blocks = NB // 2

    def some(part):
        return pl.ds(part * half_blocks, half_blocks)

    def to_rows(part, k):
        peer = lax.rem(h + k, Y)
        return pltpu.make_async_remote_copy(
            src_ref=gat.at[some(part), peer], dst_ref=gall.at[h, some(part)],
            send_sem=a1s.at[part, k], recv_sem=a1r.at[part, k],
            device_id={"head": peer}, device_id_type=MESH,
        )

    def to_columns(part, k):
        peer = lax.rem(h + k, Y)
        return pltpu.make_async_remote_copy(
            src_ref=ob.at[peer, some(part)], dst_ref=o_ref.at[some(part), h],
            send_sem=a2s.at[part, k], recv_sem=a2r.at[part, k],
            device_id={"head": peer}, device_id_type=MESH,
        )

    def keep_columns(part):
        return pltpu.make_async_copy(ob.at[h, some(part)], o_ref.at[some(part), h], a2r.at[part, 0])

    far_first = sorted(range(1, Y), key=lambda k: -min(k, Y - k))
    out_gain = og[...].astype(F32).reshape(1, -1)

    def finish(part):
        for j in range(part * half_blocks, (part + 1) * half_blocks):
            at = slice(j * BLK, (j + 1) * BLK)
            floats = att[at, :]
            centred = floats - jnp.mean(floats, axis=-1, keepdims=True)
            spread = jnp.mean(centred * centred, axis=-1, keepdims=True)
            normed = centred * lax.rsqrt(spread + EPS) * out_gain * gb[at, :].astype(F32)
            gat[j] = normed.astype(BF16).reshape(Y, share, DH)
        for k in far_first:
            to_rows(part, k).start()
        gall[h, some(part)] = gat[some(part), h]

    def mix(part):
        for k in far_first:
            to_rows(part, k).wait_recv()
        rows = half_blocks * share
        gated = jnp.concatenate(
            [gall[y, some(part)].reshape(rows, DH) for y in range(Y)], axis=1
        )
        cols = ob.shape[3]
        for y in range(Y):
            at = slice(y * cols, (y + 1) * cols)
            weights = wf[:, :, :, at].reshape(Y * DH, cols)
            summed = jnp.dot(gated, weights, preferred_element_type=F32)
            for n in range(half_blocks):
                j = part * half_blocks + n
                mine = pl.ds(pl.multiple_of(j * BLK + h * share, share), share)
                ob[y, j] = (
                    summed[n * share : (n + 1) * share] + xb[mine, at].astype(F32)
                ).astype(BF16)
        for k in far_first:
            to_columns(part, k).start()
        keep_columns(part).start()

    attend_shared(2)
    attend_shared(1)
    finish(1)
    ring_step(4)
    attend_shared(0)

    @pl.when(has_lane(3))
    def _():
        hop(2, NB - 1).wait_recv()
        scores = lax.dot_general(qb[:BLK, :], kv[3, NB - 1, 0], NT, preferred_element_type=F32)
        half = scores * scale
        kept = half * mr[0, 3 * 6 + 2 : 3 * 6 + 3, BLK:]
        weight = (kept + kept * jnp.tanh(half)).astype(BF16)
        att[:BLK, :] += jnp.dot(weight, kv[3, NB - 1, 1], preferred_element_type=F32)

    finish(0)
    for r in range(1, n_up + 1):
        share_up(r, 1 - p).wait_recv()
    for r in range(1, n_down + 1):
        share_down(r, 1 - p).wait_recv()
    mix(1)
    mix(0)

    def sent(i, carry):
        for l in range(2):

            @pl.when(has_lane(l) & ~is_last)
            def _():
                hop(l, i).wait_send()

        @pl.when(has_lane(2) & ~is_last & (p == 1))
        def _():
            third(i).wait_send()

        for k in range(3):

            @pl.when(has_lane(k + p) & (k + p <= 2))
            def _():
                push(k, i).wait_send()

        return carry

    lax.fori_loop(0, NB, sent, 0)

    @pl.when(has_lane(2) & ~is_last & (p == 0))
    def _():
        hop(2, NB - 1).wait_send()

    @pl.when(has_lane(3) & (p == 0))
    def _():
        third_shared.wait_send()

    for r in range(1, n_up + 1):
        ring_up(r).wait_send()
        share_up(r, p).wait_send()
    for r in range(1, n_down + 1):
        ring_down(r).wait_send()
        share_down(r, p).wait_send()
    for part in range(2):
        keep_columns(part).wait()
        for k in range(1, Y):
            to_rows(part, k).wait_send()
            to_columns(part, k).wait_send()
            to_columns(part, k).wait_recv()


def solution(mesh):
    S, Y = mesh.shape["seq"], mesh.shape["head"]

    def body(history, ln_gain, w_in, out_gain, w_out, block_lists, counts):
        tok, width = history.shape
        NB = tok // BLK
        cols = width // Y
        vmem = pl.BlockSpec(memory_space=pltpu.VMEM)
        hbm = pl.BlockSpec(memory_space=pltpu.HBM)
        dma = pltpu.SemaphoreType.DMA
        return pl.pallas_call(
            functools.partial(kernel, S, Y, NB),
            out_shape=jax.ShapeDtypeStruct((NB, Y, BLK // Y, cols), BF16),
            in_specs=[hbm, vmem, hbm, vmem, hbm, pl.BlockSpec(memory_space=pltpu.SMEM)],
            out_specs=vmem,
            scratch_shapes=[
                pltpu.VMEM((tok, width), BF16),
                pltpu.VMEM((tok, width), BF16),
                pltpu.VMEM((width, 2 * DH), BF16),
                pltpu.VMEM((width, 2 * DH), BF16),
                pltpu.VMEM((Y, 2, DH // 2, width), BF16),
                pltpu.VMEM((4, NB, 2, BLK, DH), BF16),
                pltpu.VMEM((3, NB, 2, BLK, DH), BF16),
                pltpu.VMEM((tok, DH), BF16),
                pltpu.VMEM((tok, DH), BF16),
                pltpu.VMEM((tok, DH), F32),
                pltpu.VMEM((NB, 24, 2 * BLK), F32),
                pltpu.VMEM((NB, Y, BLK // Y, DH), BF16),
                pltpu.VMEM((Y, NB, BLK // Y, DH), BF16),
                pltpu.VMEM((Y, NB, BLK // Y, cols), BF16),
                dma((NB,)), dma((5,)),
                dma((3, NB)), dma((3, NB)), dma((3, NB)), dma((3, NB)),
                dma((Y,)), dma((Y,)), dma((Y,)), dma((Y,)),
                dma((Y,)), dma((Y,)), dma((Y,)), dma((Y,)),
                dma((2, Y)), dma((2, Y)), dma((2, Y)), dma((2, Y)), dma((1,)),
            ],
            compiler_params=pltpu.CompilerParams(
                collective_id=0, has_side_effects=True, vmem_limit_bytes=40 * 2**20
            ),
        )(
            *(
                pltpu.with_memory_space_constraint(x, pltpu.HBM)
                for x in (
                    history, ln_gain, w_in, out_gain,
                    w_out.reshape(2, DH // 2, width), block_lists,
                )
            )
        ).reshape(tok, cols)

    placed = (
        P("seq", None),
        P(),
        P(None, None, "head"),
        P("head"),
        P("head", None),
        P("seq", None),
        P("seq"),
    )
    return jax.shard_map(
        body, mesh=mesh, in_specs=placed, out_specs=P("seq", "head"), check_vma=False
    )
```

```python
import functools

import jax
import jax.numpy as jnp
from jax import lax
from jax.experimental import pallas as pl
from jax.experimental.pallas import tpu as pltpu
from jax.sharding import PartitionSpec as P

DH = 128
BLK = 128
EPS = 1e-05
MESH = pl.DeviceIdType.MESH
F32 = jnp.float32
BF16 = jnp.bfloat16
NT = (((1,), (1,)), ((), ()))


def silu(v):
    half = 0.5 * v
    return half + half * jnp.tanh(half)


def kernel(
    S, Y, NB,
    hist, lng, win, og, wout, lists, o_ref,
    xb, nb, wkv, wqg, wf, kv, sv, qb, gb, att, mr, gat, gall, ob,
    in_sem, w_sem, xs, xr, ps, pr, rs, rr, ls, lr, bs, br, a1s, a1r, a2s, a2r, fs,
):
    share = BLK // Y
    s = lax.axis_index("seq")
    h = lax.axis_index("head")
    p = lax.rem(s, 2)
    chip = lax.div(s, 2)
    is_first, is_last = chip == 0, chip == S // 2 - 1
    nxt = jnp.minimum(s + 2, S - 1)
    prv = jnp.maximum(s - 2, 0)
    sib = s + 1 - 2 * p
    scale = 0.5 * DH ** (-0.5)

    def block_rows(i):
        return pl.ds(pl.multiple_of(i * BLK, BLK), BLK)

    def load_block(i):
        return pltpu.make_async_copy(hist.at[block_rows(i)], xb.at[block_rows(i)], in_sem.at[i])

    def load_w(which, dst, half, sem):
        return pltpu.make_async_copy(
            win.at[which], dst.at[:, pl.ds(half * DH, DH)], w_sem.at[sem]
        )

    loads = [load_w(3, wkv, 0, 0), load_w(1, wkv, 1, 1), load_w(2, wqg, 0, 2), load_w(0, wqg, 1, 3)]
    half_rows = DH // 2
    load_out = pltpu.make_async_copy(wout, wf.at[h], w_sem.at[4])
    load_block(NB - 1).start()
    loads[0].start()
    loads[1].start()
    load_out.start()
    for i in range(NB - 2, -1, -1):
        load_block(i).start()
    loads[2].start()
    loads[3].start()

    barrier = pltpu.get_barrier_semaphore()
    pl.semaphore_signal(barrier, inc=1, device_id={"seq": sib}, device_id_type=MESH)

    @pl.when(~is_first)
    def _():
        pl.semaphore_signal(barrier, inc=1, device_id={"seq": prv}, device_id_type=MESH)

    @pl.when(~is_first & (p == 0))
    def _():
        pl.semaphore_signal(
            barrier, inc=1, device_id={"seq": jnp.maximum(s - 1, 0)}, device_id_type=MESH
        )

    for k in range(1, Y):
        pl.semaphore_signal(
            barrier, inc=1, device_id={"head": lax.rem(h + k, Y)}, device_id_type=MESH
        )

    def hop(l, i):
        return pltpu.make_async_remote_copy(
            src_ref=kv.at[l, i], dst_ref=kv.at[l + 1, i],
            send_sem=xs.at[l, i], recv_sem=xr.at[l, i],
            device_id={"seq": nxt}, device_id_type=MESH,
        )

    def push(k, i):
        return pltpu.make_async_remote_copy(
            src_ref=kv.at[k + p, i], dst_ref=sv.at[k, i],
            send_sem=ps.at[k, i], recv_sem=pr.at[k, i],
            device_id={"seq": sib}, device_id_type=MESH,
        )

    def third(i):
        return pltpu.make_async_remote_copy(
            src_ref=kv.at[2, i], dst_ref=sv.at[2, i],
            send_sem=xs.at[2, i], recv_sem=pr.at[2, i],
            device_id={"seq": jnp.minimum(s + 1, S - 1)}, device_id_type=MESH,
        )

    third_shared = pltpu.make_async_remote_copy(
        src_ref=sv.at[2, NB - 1], dst_ref=kv.at[3, NB - 1],
        send_sem=fs.at[0], recv_sem=xr.at[2, NB - 1],
        device_id={"seq": sib}, device_id_type=MESH,
    )

    def place(k):
        return lax.rem(h + k + Y, Y)

    near = (1, -1, 2, -2)

    def gather_near(n):
        return pltpu.make_async_remote_copy(
            src_ref=wf.at[h, p], dst_ref=wf.at[h, p],
            send_sem=rs.at[n], recv_sem=rr.at[n],
            device_id={"head": place(near[n])}, device_id_type=MESH,
        )

    def gather_far(n):
        sign = 1 if n % 2 == 0 else -1
        shard = wf.at[place(-2 * sign), p]
        if n >= 2:
            shard = shard.at[pl.ds((n - 2) * (half_rows // 2), half_rows // 2)]
        return pltpu.make_async_remote_copy(
            src_ref=shard, dst_ref=shard,
            send_sem=ls.at[n], recv_sem=lr.at[n],
            device_id={"head": place(sign if n < 2 else 2 * sign)}, device_id_type=MESH,
        )

    def share_half(k, half):
        shard = wf.at[place(k), half]
        return pltpu.make_async_remote_copy(
            src_ref=shard, dst_ref=shard,
            send_sem=bs.at[k], recv_sem=br.at[k],
            device_id={"seq": sib}, device_id_type=MESH,
        )

    def gather_start():
        for n in range(4):
            gather_near(n).start()

    def gather_middle():
        for n in range(4):
            gather_near(n).wait_recv()
        for n in range(4):
            gather_far(n).start()
        for k in (1, 2, Y - 1, Y - 2):
            share_half(k, p).start()

    def gather_end():
        for n in range(4):
            gather_far(n).wait_recv()
        for k in (3, 4, 5):
            share_half(k, p).start()

    loads[0].wait()
    loads[1].wait()
    gain = lng[...].astype(F32).reshape(1, -1)

    def project(n, carry):
        i = NB - 1 - n
        load_block(i).wait()
        for piece in range(4):
            at = pl.ds(pl.multiple_of(i * BLK + piece * 32, 32), 32)
            floats = xb[at, :].astype(F32)
            centred = floats - jnp.mean(floats, axis=-1, keepdims=True)
            spread = jnp.mean(centred * centred, axis=-1, keepdims=True)
            nb[at, :] = (centred * lax.rsqrt(spread + EPS) * gain).astype(BF16)
        both = silu(jnp.dot(nb[block_rows(i), :], wkv[...], preferred_element_type=F32)).astype(BF16)
        kv[0, i, 0] = both[:, :DH]
        kv[0, i, 1] = both[:, DH:]

        @pl.when(n == 0)
        def _():
            pl.semaphore_wait(barrier, Y + (chip < S // 2 - 1).astype(jnp.int32) * (1 + p))

        @pl.when(~is_last)
        def _():
            hop(0, i).start()

        @pl.when(p == 0)
        def _():
            push(0, i).start()

        @pl.when(n == 0)
        def _():
            load_out.wait()
            gather_start()

        return carry

    lax.fori_loop(0, NB, project, 0)

    loads[2].wait()
    loads[3].wait()

    def project_q(i, carry):
        both = silu(jnp.dot(nb[block_rows(i), :], wqg[...], preferred_element_type=F32)).astype(BF16)
        qb[block_rows(i), :] = both[:, :DH]
        gb[block_rows(i), :] = both[:, DH:]
        return carry

    lax.fori_loop(0, NB, project_q, 0)

    shape = mr.shape[1:]
    row = lax.broadcasted_iota(jnp.int32, shape, 0)
    lane = lax.broadcasted_iota(jnp.int32, shape, 1)
    back = (row * 11) >> 5
    key_id = NB * (s - back) + 2 * (row - 3 * back) + (lane >> 7)
    for j in range(NB):
        listed = key_id == lists[j, 0]
        for k in range(1, lists.shape[1]):
            listed = listed | (key_id == lists[j, k])
        mr[j] = jnp.where(listed, 1.0, 0.0)

    def attend(keys, values, at, first, t_own):
        scores = lax.dot_general(qb[first * BLK :, :], keys, NT, preferred_element_type=F32)
        pieces = []
        for j in range(first, NB):
            half = scores[(j - first) * BLK : (j - first + 1) * BLK] * scale
            keep = mr[j, pl.ds(at, 1), :]
            kept = half * keep
            weight = kept + kept * jnp.tanh(half)
            if t_own is not None and j <= 2 * t_own + 1:
                q_at = j * BLK + lax.broadcasted_iota(jnp.int32, weight.shape, 0)
                k_at = 2 * t_own * BLK + lax.broadcasted_iota(jnp.int32, weight.shape, 1)
                weight = jnp.where(k_at <= q_at, weight, 0.0)
            pieces.append(weight.astype(BF16))
        weights = jnp.concatenate(pieces, axis=0)
        update = jnp.dot(weights, values, preferred_element_type=F32)
        if t_own == 0:
            att[...] = update
        else:
            att[first * BLK :, :] += update

    def pair(buf, l, t):
        blocks = pl.ds(2 * t, 2)
        return buf[l, blocks, 0].reshape(2 * BLK, DH), buf[l, blocks, 1].reshape(2 * BLK, DH)

    for t in range(NB // 2):
        keys, values = pair(kv, 0, t)
        attend(keys, values, t, 2 * t, t)

    def has_lane(l):
        return chip >= l

    def has_shared(k):
        return chip + p >= k + 1

    def middle(n, carry):
        l = 1 + n // 3
        t = 2 - lax.rem(n, 3)

        @pl.when(has_lane(l))
        def _():
            for i in (2 * t + 1, 2 * t):
                hop(l - 1, i).wait_recv()

                @pl.when(((l == 1) | ((p == 0) & (i == NB - 1))) & ~is_last)
                def _():
                    hop(l, i).start()

                @pl.when((l == 2) & (p == 1) & ~is_last)
                def _():
                    third(i).start()

                push(l - p, i).start()


        @pl.when(has_lane(l))
        def _():
            keys, values = pair(kv, l, t)
            attend(keys, values, 3 * (2 * l) + t, 0, None)

        @pl.when(has_shared(l - 1))
        def _():
            for i in (2 * t + 1, 2 * t):
                push(l - 1, i).wait_recv()
            keys, values = pair(sv, l - 1, t)
            attend(keys, values, 3 * (2 * l - 1) + t, 0, None)

        @pl.when(n == 3)
        def _():
            gather_middle()

        return carry

    lax.fori_loop(0, 6, middle, 0)

    def attend_shared(t):
        @pl.when(has_shared(2))
        def _():
            for i in (2 * t + 1, 2 * t):
                push(2, i).wait_recv()
                if i == NB - 1:

                    @pl.when(p == 0)
                    def _():
                        third_shared.start()

            keys, values = pair(sv, 2, t)
            attend(keys, values, 3 * 5 + t, 0, None)

    half_blocks = NB // 2

    def some(part):
        return pl.ds(part * half_blocks, half_blocks)

    def to_rows(part, k):
        peer = lax.rem(h + k, Y)
        return pltpu.make_async_remote_copy(
            src_ref=gat.at[some(part), peer], dst_ref=gall.at[h, some(part)],
            send_sem=a1s.at[part, k], recv_sem=a1r.at[part, k],
            device_id={"head": peer}, device_id_type=MESH,
        )

    def to_columns(part, k):
        peer = lax.rem(h + k, Y)
        return pltpu.make_async_remote_copy(
            src_ref=ob.at[peer, some(part)], dst_ref=o_ref.at[some(part), h],
            send_sem=a2s.at[part, k], recv_sem=a2r.at[part, k],
            device_id={"head": peer}, device_id_type=MESH,
        )

    def keep_columns(part):
        return pltpu.make_async_copy(ob.at[h, some(part)], o_ref.at[some(part), h], a2r.at[part, 0])

    far_first = sorted(range(1, Y), key=lambda k: -min(k, Y - k))
    out_gain = og[...].astype(F32).reshape(1, -1)

    def finish(part):
        for j in range(part * half_blocks, (part + 1) * half_blocks):
            at = slice(j * BLK, (j + 1) * BLK)
            floats = att[at, :]
            centred = floats - jnp.mean(floats, axis=-1, keepdims=True)
            spread = jnp.mean(centred * centred, axis=-1, keepdims=True)
            normed = centred * lax.rsqrt(spread + EPS) * out_gain * gb[at, :].astype(F32)
            gat[j] = normed.astype(BF16).reshape(Y, share, DH)
        for k in far_first:
            to_rows(part, k).start()
        gall[h, some(part)] = gat[some(part), h]

    def mix(part):
        for k in far_first:
            to_rows(part, k).wait_recv()
        rows = half_blocks * share
        gated = jnp.concatenate(
            [gall[y, some(part)].reshape(rows, DH) for y in range(Y)], axis=1
        )
        cols = ob.shape[3]
        for y in range(Y):
            at = slice(y * cols, (y + 1) * cols)
            weights = wf[:, :, :, at].reshape(Y * DH, cols)
            summed = jnp.dot(gated, weights, preferred_element_type=F32)
            for n in range(half_blocks):
                j = part * half_blocks + n
                mine = pl.ds(pl.multiple_of(j * BLK + h * share, share), share)
                ob[y, j] = (
                    summed[n * share : (n + 1) * share] + xb[mine, at].astype(F32)
                ).astype(BF16)
        for k in far_first:
            to_columns(part, k).start()
        keep_columns(part).start()

    attend_shared(2)
    attend_shared(1)
    finish(1)
    gather_end()
    attend_shared(0)

    @pl.when(has_lane(3))
    def _():
        hop(2, NB - 1).wait_recv()
        scores = lax.dot_general(qb[:BLK, :], kv[3, NB - 1, 0], NT, preferred_element_type=F32)
        half = scores * scale
        kept = half * mr[0, 3 * 6 + 2 : 3 * 6 + 3, BLK:]
        weight = (kept + kept * jnp.tanh(half)).astype(BF16)
        att[:BLK, :] += jnp.dot(weight, kv[3, NB - 1, 1], preferred_element_type=F32)

    finish(0)
    for k in range(1, Y):
        share_half(k, 1 - p).wait_recv()
    mix(1)
    mix(0)

    def sent(i, carry):
        for l in range(2):

            @pl.when(has_lane(l) & ~is_last)
            def _():
                hop(l, i).wait_send()

        @pl.when(has_lane(2) & ~is_last & (p == 1))
        def _():
            third(i).wait_send()

        for k in range(3):

            @pl.when(has_lane(k + p) & (k + p <= 2))
            def _():
                push(k, i).wait_send()

        return carry

    lax.fori_loop(0, NB, sent, 0)

    @pl.when(has_lane(2) & ~is_last & (p == 0))
    def _():
        hop(2, NB - 1).wait_send()

    @pl.when(has_lane(3) & (p == 0))
    def _():
        third_shared.wait_send()

    for n in range(4):
        gather_near(n).wait_send()
        gather_far(n).wait_send()
    for k in range(1, Y):
        share_half(k, p).wait_send()
    for part in range(2):
        keep_columns(part).wait()
        for k in range(1, Y):
            to_rows(part, k).wait_send()
            to_columns(part, k).wait_send()
            to_columns(part, k).wait_recv()


def solution(mesh):
    S, Y = mesh.shape["seq"], mesh.shape["head"]

    def body(history, ln_gain, w_in, out_gain, w_out, block_lists, counts):
        tok, width = history.shape
        NB = tok // BLK
        cols = width // Y
        vmem = pl.BlockSpec(memory_space=pltpu.VMEM)
        hbm = pl.BlockSpec(memory_space=pltpu.HBM)
        dma = pltpu.SemaphoreType.DMA
        return pl.pallas_call(
            functools.partial(kernel, S, Y, NB),
            out_shape=jax.ShapeDtypeStruct((NB, Y, BLK // Y, cols), BF16),
            in_specs=[hbm, vmem, hbm, vmem, hbm, pl.BlockSpec(memory_space=pltpu.SMEM)],
            out_specs=vmem,
            scratch_shapes=[
                pltpu.VMEM((tok, width), BF16),
                pltpu.VMEM((tok, width), BF16),
                pltpu.VMEM((width, 2 * DH), BF16),
                pltpu.VMEM((width, 2 * DH), BF16),
                pltpu.VMEM((Y, 2, DH // 2, width), BF16),
                pltpu.VMEM((4, NB, 2, BLK, DH), BF16),
                pltpu.VMEM((3, NB, 2, BLK, DH), BF16),
                pltpu.VMEM((tok, DH), BF16),
                pltpu.VMEM((tok, DH), BF16),
                pltpu.VMEM((tok, DH), F32),
                pltpu.VMEM((NB, 24, 2 * BLK), F32),
                pltpu.VMEM((NB, Y, BLK // Y, DH), BF16),
                pltpu.VMEM((Y, NB, BLK // Y, DH), BF16),
                pltpu.VMEM((Y, NB, BLK // Y, cols), BF16),
                dma((NB,)), dma((5,)),
                dma((3, NB)), dma((3, NB)), dma((3, NB)), dma((3, NB)),
                dma((4,)), dma((4,)), dma((4,)), dma((4,)), dma((Y,)), dma((Y,)),
                dma((2, Y)), dma((2, Y)), dma((2, Y)), dma((2, Y)), dma((1,)),
            ],
            compiler_params=pltpu.CompilerParams(
                collective_id=0, has_side_effects=True, vmem_limit_bytes=40 * 2**20
            ),
        )(
            *(
                pltpu.with_memory_space_constraint(x, pltpu.HBM)
                for x in (
                    history, ln_gain, w_in, out_gain,
                    w_out.reshape(2, DH // 2, width), block_lists,
                )
            )
        ).reshape(tok, cols)

    placed = (
        P("seq", None),
        P(),
        P(None, None, "head"),
        P("head"),
        P("head", None),
        P("seq", None),
        P("seq"),
    )
    return jax.shard_map(
        body, mesh=mesh, in_specs=placed, out_specs=P("seq", "head"), check_vma=False
    )
```
